32 devices in a mesh: section: 2 (over y), fsdp: 16 (over z, x, core).
Axes of the slice: x: 2, y: 2, z: 4, core: 2. Of those that a mesh axis runs over, the one named last changes fastest.
Arguments:
- tokens: bfloat16 [2, 2048, 1536], P(None, 'fsdp'), may hold values from -6 to 6
- cotangent: float32 [2, 2048, 1536], P(None, 'fsdp'), may hold values from -6 to 6
- in_weight: bfloat16 [2, 1536, 6448], P('section', 'fsdp'), may hold values from -0.15625 to 0.15625
- out_weight: bfloat16 [2, 3072, 1536], P('section', 'fsdp'), may hold values from -0.109375 to 0.109375
- norm_gain: float32 [2, 1536], P('section'), may hold values from 0.1 to 1.9
- conv_weight: float32 [2, 4, 3328], P('section'), may hold values from -0.6 to 0.6
- conv_bias: float32 [2, 3328], P('section'), may hold values from -0.5 to 0.5
- step_bias: float32 [2, 48], P('section'), may hold values from -3 to -1
- decay_log: float32 [2, 48], P('section'), may hold values from -4 to 1
- skip_gain: float32 [2, 48], P('section'), may hold values from 0.5 to 1.5
- gate_gain: float32 [2, 3072], P('section'), may hold values from 0.1 to 1.9
- seq_starts: int32 [2, 2048], P(None, 'fsdp'), may hold values from 0 to 1, as said below
Outputs:
- layer_out: bfloat16 [2, 2, 2048, 1536], P('section', None, 'fsdp')
- in_grad: float32 [2, 2, 2048, 1536], P('section', None, 'fsdp')
- in_weight_grad: float32 [2, 1536, 6448], P('section', 'fsdp')
- out_weight_grad: float32 [2, 3072, 1536], P('section', 'fsdp')
- norm_gain_grad: float32 [2, 1536], P('section')
- conv_weight_grad: float32 [2, 4, 3328], P('section')
- conv_bias_grad: float32 [2, 3328], P('section')
- step_bias_grad: float32 [2, 48], P('section')
- decay_log_grad: float32 [2, 48], P('section')
- skip_gain_grad: float32 [2, 48], P('section')
- gate_gain_grad: float32 [2, 3072], P('section')
The draws below stay inside these ranges and needn't reach their ends.
Inputs may be any that keep to these rules, and one draw needn't show every extreme that they name: `seq_starts`: the first token of each aligned block of 128 tokens (the tokens of one device) begins a sequence, so no sequence is longer than 128.
All inputs are finite; a program needn't handle non-finite values.
Results may differ from the reference program's by a relative error of at most 0.012.
The reference program's roundings to bfloat16 on the way count: a program that leaves them out, or rounds other values in their place, can miss the bound.
Values may be sent and summed in bfloat16 or wider, within the bound.
No kernel may reach another device: no remote copies, remote signals or barrier semaphores. Data moves between devices by JAX's collectives and lax.ppermute only.
A program may use at most 384 MiB of HBM per device.

```python
import jax
import jax.numpy as jnp
from jax import lax

D = 1536
INNER = 3072
HEADS = 48
HEAD_DIM = 64
STATE = 128
CONV = 4
GROUP = 256
TOK_DEV = 128
MICRO = 2
CONV_CH = 3328
IN_W = 6448
TOKENS = 2048
N_SECTION = 2
N_FSDP = 16


def draw_seq_starts(key, part):
    positions = jnp.arange(TOKENS)
    rolled = jax.random.randint(key, (MICRO, TOKENS), 0, 96)
    block_first = (positions % TOK_DEV == 0)[None, :]
    return jnp.where(block_first | (rolled == 0), 1, 0).astype(jnp.int32)


def block_levels(key, extent, shards, least, top_value):
    loudness, own = 1.0, jax.random.fold_in(key, 6)
    for dim, shards_of in shards:
        heights = jnp.exp(jax.random.uniform(jax.random.fold_in(own, dim), (shards_of,), jnp.float32, least / len(shards), top_value / len(shards)))
        loudness = loudness * jnp.repeat(heights, extent[dim] // shards_of).reshape([-1 if axis == dim else 1 for axis in range(len(extent))])
    return loudness


def noise(stream_key, shape, width, bound, shards=(), kind=jnp.bfloat16):
    array = jax.random.normal(stream_key, shape, jnp.float32) * width
    if len(shards) > 0:
        array = block_levels(stream_key, shape, shards, -0.22, 0.18) * array
    return jnp.clip(array, min=-bound, max=bound).astype(kind)


def setup_inputs(seed: int = 0) -> dict:
    keys = jax.random.split(jax.random.key(seed), 13)
    tokens = noise(keys[0], (MICRO, TOKENS, D), 1.0, 6.0, ((1, 16),))
    cotangent = noise(keys[1], (MICRO, TOKENS, D), 1.0, 6.0, ((1, 16),), jnp.float32)
    in_weight = noise(keys[2], (N_SECTION, D, IN_W), D ** -0.5, 0.15625, ((0, 2), (1, 16)))
    out_weight = noise(keys[3], (N_SECTION, INNER, D), INNER ** -0.5, 0.109375, ((0, 2), (1, 16)))
    norm_gain = jnp.clip(1.0 + 0.18 * jax.random.normal(keys[4], (N_SECTION, D), jnp.float32), 0.1, 1.9)
    conv_weight = jnp.clip(jax.random.uniform(keys[5], (N_SECTION, CONV, CONV_CH), jnp.float32, -0.6, 0.6) * block_levels(keys[5], (N_SECTION, CONV, CONV_CH), ((0, 2),), -0.4, 0.0), -0.6, 0.6)
    conv_bias = jnp.clip(jax.random.uniform(keys[6], (N_SECTION, CONV_CH), jnp.float32, -0.5, 0.5) * block_levels(keys[6], (N_SECTION, CONV_CH), ((0, 2),), -0.4, 0.0), -0.5, 0.5)
    step_bias = jnp.clip(-3.0 + 2.0 * jax.random.uniform(keys[7], (N_SECTION, HEADS), jnp.float32) ** block_levels(keys[7], (N_SECTION, HEADS), ((0, 2),), -0.2, 0.2), -3.0, -1.0)
    decay_log = jnp.clip(-4.0 + 5.0 * jax.random.uniform(keys[8], (N_SECTION, HEADS), jnp.float32) ** block_levels(keys[8], (N_SECTION, HEADS), ((0, 2),), -0.2, 0.2), -4.0, 1.0)
    skip_gain = jnp.clip(0.5 + 1.0 * jax.random.uniform(keys[9], (N_SECTION, HEADS), jnp.float32) ** block_levels(keys[9], (N_SECTION, HEADS), ((0, 2),), -0.2, 0.2), 0.5, 1.5)
    gate_gain = jnp.clip(1.0 + 0.18 * jax.random.normal(keys[10], (N_SECTION, INNER), jnp.float32), 0.1, 1.9)
    seq_starts = draw_seq_starts(jax.random.fold_in(keys[12], 71), 0)
    return {"tokens": tokens, "cotangent": cotangent, "in_weight": in_weight, "out_weight": out_weight, "norm_gain": norm_gain, "conv_weight": conv_weight, "conv_bias": conv_bias, "step_bias": step_bias, "decay_log": decay_log, "skip_gain": skip_gain, "gate_gain": gate_gain, "seq_starts": seq_starts}


norm_eps = 1e-05
top_precision = lax.Precision.HIGHEST

def norm_map(stream, norm_gain):
    return stream * lax.rsqrt(lax.optimization_barrier(jnp.mean(stream * stream, axis=-1, keepdims=True)) + norm_eps) * norm_gain[None, :]

def causal_conv(conv_input, segment, conv_weight, conv_bias):
    row_count = conv_input.shape[0]
    summed = conv_bias[None, :] + conv_weight[CONV - 1][None, :] * conv_input
    for offset in range(1, CONV):
        earlier = jnp.pad(conv_input, ((offset, 0), (0, 0)))[:row_count]
        earlier_seg = jnp.pad(segment, (offset, 0), constant_values=-1)[:row_count]
        matching = (earlier_seg == segment).astype(jnp.float32)[:, None]
        summed = summed + conv_weight[CONV - 1 - offset][None, :] * earlier * matching
    return jax.nn.silu(summed)

def ssd_mix(projected, seq_starts, conv_weight, conv_bias, step_bias, decay_log, skip_gain, gate_gain):
    row_count = projected.shape[0]
    span = min(GROUP, row_count)
    blocks = row_count // span
    gate_part = projected[:, :INNER]
    conv_input = projected[:, INNER:INNER + CONV_CH]
    step_input = projected[:, INNER + CONV_CH:]
    segment = jnp.cumsum(seq_starts).astype(jnp.int32)
    activated = causal_conv(conv_input, segment, conv_weight, conv_bias)
    head_values = activated[:, :INNER].reshape(blocks, span, HEADS, HEAD_DIM)
    in_state = activated[:, INNER:INNER + STATE].reshape(blocks, span, STATE)
    out_state = activated[:, INNER + STATE:].reshape(blocks, span, STATE)
    step_size = jax.nn.softplus(step_input + step_bias[None, :])
    log_decay = -jnp.exp(decay_log)[None, :] * step_size
    step_heads = step_size.reshape(blocks, span, HEADS).transpose(0, 2, 1)
    cum_decay = jnp.cumsum(log_decay.reshape(blocks, span, HEADS), axis=1).transpose(0, 2, 1)
    seg_blocks = segment.reshape(blocks, span)
    start_blocks = seq_starts.reshape(blocks, span)
    positions = jnp.arange(span)
    causal = (positions[:, None] >= positions[None, :])[None] & (seg_blocks[:, :, None] == seg_blocks[:, None, :])
    log_gap = cum_decay[:, :, :, None] - cum_decay[:, :, None, :]
    within = jnp.exp(jnp.where(causal[:, None], log_gap, -jnp.inf))
    scores = jnp.einsum('bin,bjn->bij', out_state, in_state, precision=top_precision)
    mixing = within * scores[:, None] * step_heads[:, :, None, :]
    intra = jnp.einsum('bhij,bjhp->bihp', mixing, head_values, precision=top_precision)
    same_end = (seg_blocks == seg_blocks[:, -1:]).astype(jnp.float32)
    to_end = jnp.exp(cum_decay[:, :, -1:] - cum_decay) * same_end[:, None, :] * step_heads
    states = jnp.einsum('bhj,bjn,bjhp->bhpn', to_end, in_state, head_values, precision=top_precision)
    carry_keep = (lax.optimization_barrier(jnp.sum(start_blocks, axis=1)) == 0).astype(jnp.float32)
    block_decay = jnp.exp(cum_decay[:, :, -1]) * carry_keep[:, None]

    def advance(entering, item):
        block_state, factor = item
        return (entering * factor[:, None, None] + block_state, entering)
    _, entering = lax.scan(advance, jnp.zeros((HEADS, HEAD_DIM, STATE), jnp.float32), (states, block_decay))
    before_start = (jnp.cumsum(start_blocks, axis=1) == 0).astype(jnp.float32)
    from_start = jnp.exp(cum_decay) * before_start[:, None, :]
    carried_in = jnp.einsum('bin,bhpn,bhi->bihp', out_state, entering, from_start, precision=top_precision)
    mixed_heads = intra + carried_in + skip_gain[None, None, :, None] * head_values
    gated = mixed_heads.reshape(row_count, INNER) * jax.nn.silu(gate_part)
    return gated * lax.rsqrt(lax.optimization_barrier(jnp.mean(gated * gated, axis=-1, keepdims=True)) + norm_eps) * gate_gain[None, :]

def layer_forward(layer_in, in_full, out_full, small_params, seq_starts):
    stream = layer_in.astype(jnp.float32)
    normed = norm_map(stream, small_params[0]).astype(jnp.bfloat16)
    projected = jnp.dot(normed, in_full, preferred_element_type=jnp.float32)
    mixed_out = ssd_mix(projected, seq_starts, small_params[1], small_params[2], small_params[3], small_params[4], small_params[5], small_params[6]).astype(jnp.bfloat16)
    result = (stream + jnp.dot(mixed_out, out_full, preferred_element_type=jnp.float32)).astype(jnp.bfloat16)
    return (result, (normed, projected, mixed_out))

def layer_backward(layer_in, kept_acts, in_full, out_full, small_params, seq_starts, upstream):
    normed, projected, mixed_out = kept_acts
    upstream_bf = upstream.astype(jnp.bfloat16)
    grad_out_w = jnp.dot(mixed_out.T, upstream_bf, preferred_element_type=jnp.float32)
    grad_mixed = jnp.dot(upstream_bf, out_full.T, preferred_element_type=jnp.float32)

    def mixer_only(proj_arg, conv_w, conv_b, step_b, decay_l, skip_g, gate_g):
        return ssd_mix(proj_arg, seq_starts, conv_w, conv_b, step_b, decay_l, skip_g, gate_g)
    _, mixer_pull = jax.vjp(mixer_only, projected, small_params[1], small_params[2], small_params[3], small_params[4], small_params[5], small_params[6])
    pulled = mixer_pull(grad_mixed)
    grad_proj_bf = pulled[0].astype(jnp.bfloat16)
    grad_in_w = jnp.dot(normed.T, grad_proj_bf, preferred_element_type=jnp.float32)
    grad_normed = jnp.dot(grad_proj_bf, in_full.T, preferred_element_type=jnp.float32)
    _, norm_pull = jax.vjp(norm_map, layer_in.astype(jnp.float32), small_params[0])
    grad_stream, grad_gain = norm_pull(grad_normed)
    return (upstream + grad_stream, grad_in_w, grad_out_w, (grad_gain,) + tuple(pulled[1:]))

def reference(tokens, cotangent, in_weight, out_weight, norm_gain, conv_weight, conv_bias, step_bias, decay_log, skip_gain, gate_gain, seq_starts):
    params_all = (norm_gain, conv_weight, conv_bias, step_bias, decay_log, skip_gain, gate_gain)
    first_small = tuple((p[0] for p in params_all))
    second_small = tuple((p[1] for p in params_all))
    count = MICRO * N_FSDP
    tok_blocks = tokens.reshape(count, TOK_DEV, D)
    cot_blocks = cotangent.reshape(count, TOK_DEV, D)
    start_blocks = seq_starts.reshape(count, TOK_DEV)

    def one_block(carry, item):
        block_in, block_cot, block_starts = item
        first_out, first_kept = layer_forward(block_in, in_weight[0], out_weight[0], first_small, block_starts)
        second_out, second_kept = layer_forward(first_out, in_weight[1], out_weight[1], second_small, block_starts)
        grad_mid, in_w1, out_w1, small1 = layer_backward(first_out, second_kept, in_weight[1], out_weight[1], second_small, block_starts, block_cot)
        grad_first, in_w0, out_w0, small0 = layer_backward(block_in, first_kept, in_weight[0], out_weight[0], first_small, block_starts, grad_mid)
        acc_in, acc_out, acc_small = carry
        acc_in = acc_in + jnp.stack([in_w0, in_w1])
        acc_out = acc_out + jnp.stack([out_w0, out_w1])
        acc_small = tuple((a + jnp.stack([g0, g1]) for a, g0, g1 in zip(acc_small, small0, small1)))
        return ((acc_in, acc_out, acc_small), (first_out, second_out, grad_first, grad_mid))
    start = (jnp.zeros(in_weight.shape, jnp.float32), jnp.zeros(out_weight.shape, jnp.float32), tuple((jnp.zeros(p.shape, jnp.float32) for p in params_all)))
    (acc_in, acc_out, acc_small), outs_all = lax.scan(one_block, start, (tok_blocks, cot_blocks, start_blocks))
    first_out, second_out, grad_first, grad_mid = outs_all
    layer_out = jnp.stack([first_out.reshape(MICRO, TOKENS, D), second_out.reshape(MICRO, TOKENS, D)])
    in_grad = jnp.stack([grad_first.reshape(MICRO, TOKENS, D), grad_mid.reshape(MICRO, TOKENS, D)])
    return (layer_out, in_grad, acc_in, acc_out, acc_small[0], acc_small[1], acc_small[2], acc_small[3], acc_small[4], acc_small[5], acc_small[6])
```

```python
import jax
import jax.numpy as jnp
from jax import lax
from jax.sharding import PartitionSpec as P

INNER = 3072
HEADS = 48
HEAD_DIM = 64
STATE = 128
CONV = 4
CONV_CH = 3328

norm_eps = 1e-05
top_precision = lax.Precision.HIGHEST


class Grid:
    def __init__(self, count):
        self.count = count
        self.ring = count // 4
        ident = lax.axis_index("fsdp")
        self.core = ident % 2
        self.pair = (ident // 2) % 2
        self.pos = ident // 4

    def core_swap(self, v):
        return lax.ppermute(v, "fsdp", [(i, i ^ 1) for i in range(self.count)])

    def pair_swap(self, v):
        return lax.ppermute(v, "fsdp", [(i, i ^ 2) for i in range(self.count)])

    def ring_shift(self, v):
        return lax.ppermute(v, "fsdp", [(i, (i + 4) % self.count) for i in range(self.count)])

    def block(self, back, dpair, dcore):
        pos = (self.pos + self.ring - back) % self.ring
        pair = 1 - self.pair if dpair else self.pair
        core = 1 - self.core if dcore else self.core
        return pos * 4 + pair * 2 + core

    def gather(self, shard, light=False):
        rows = shard.shape[0]
        own = [shard]
        for _ in range(self.ring - 1):
            own.append(self.ring_shift(own[-1]))
        other = []
        for k in range(self.ring):
            if light and k == 1:
                other.append(self.ring_shift(other[0]))
            else:
                other.append(self.pair_swap(own[k]))
        full = jnp.zeros((self.count * rows, shard.shape[1]), shard.dtype)
        for k in range(self.ring):
            for dpair, blk in ((0, own[k]), (1, other[k])):
                swapped = self.core_swap(blk)
                full = lax.dynamic_update_slice(full, blk, (self.block(k, dpair, 0) * rows, 0))
                full = lax.dynamic_update_slice(full, swapped, (self.block(k, dpair, 1) * rows, 0))
        return full

    def scatter(self, left_t, right, rows):
        def part(back, dpair, dcore):
            lhs = lax.dynamic_slice_in_dim(left_t, self.block(back, dpair, dcore) * rows, rows, 0)
            return jnp.dot(lhs, right, preferred_element_type=jnp.float32)

        def local(back):
            far = part(back, 1, 0) + self.core_swap(part(back, 1, 1).astype(jnp.bfloat16))
            near = part(back, 0, 0) + self.core_swap(part(back, 0, 1).astype(jnp.bfloat16))
            return near + self.pair_swap(far.astype(jnp.bfloat16))

        moving = None
        for step in range(1, self.ring):
            total = local(step)
            if moving is not None:
                total = total + moving
            moving = self.ring_shift(total.astype(jnp.bfloat16))
        return local(0) + moving

    def total(self, v):
        bit = 1
        while bit < self.count:
            v = v + lax.ppermute(v, "fsdp", [(i, i ^ bit) for i in range(self.count)])
            bit *= 2
        return v


def norm_map(stream, norm_gain):
    return (
        stream
        * lax.rsqrt(jnp.mean(stream * stream, axis=-1, keepdims=True) + norm_eps)
        * norm_gain[None, :]
    )


def causal_conv(conv_input, segment, conv_weight, conv_bias):
    row_count = conv_input.shape[0]
    summed = conv_bias[None, :] + conv_weight[CONV - 1][None, :] * conv_input
    for offset in range(1, CONV):
        earlier = jnp.pad(conv_input, ((offset, 0), (0, 0)))[:row_count]
        earlier_seg = jnp.pad(segment, (offset, 0), constant_values=-1)[:row_count]
        matching = (earlier_seg == segment).astype(jnp.float32)[:, None]
        summed = summed + conv_weight[CONV - 1 - offset][None, :] * earlier * matching
    return jax.nn.silu(summed)


def ssd_mix(
    gate_part, conv_part, seq_starts, conv_weight, conv_bias, step_bias, decay_log, skip_gain, gate_gain
):
    span = gate_part.shape[0]
    conv_input = conv_part[:, :CONV_CH]
    step_input = conv_part[:, CONV_CH:]
    segment = jnp.cumsum(seq_starts)
    activated = causal_conv(conv_input, segment, conv_weight, conv_bias)
    head_values = activated[:, :INNER].reshape(span, HEADS, HEAD_DIM)
    in_state = activated[:, INNER : INNER + STATE]
    out_state = activated[:, INNER + STATE :]
    step_size = jax.nn.softplus(step_input + step_bias[None, :])
    log_decay = -jnp.exp(decay_log)[None, :] * step_size
    step_heads = step_size.T
    cum_decay = jnp.cumsum(log_decay, axis=0).T
    positions = jnp.arange(span)
    causal = (positions[:, None] >= positions[None, :]) & (segment[:, None] == segment[None, :])
    log_gap = cum_decay[:, :, None] - cum_decay[:, None, :]
    within = jnp.exp(jnp.where(causal[None], log_gap, -jnp.inf))
    scores = jnp.einsum("in,jn->ij", out_state, in_state, precision=top_precision)
    mixing = within * scores[None] * step_heads[:, None, :]
    intra = jnp.einsum("hij,jhp->ihp", mixing, head_values, precision=top_precision)
    mixed_heads = intra + skip_gain[None, :, None] * head_values
    gated = mixed_heads.reshape(span, INNER) * jax.nn.silu(gate_part)
    return (
        gated
        * lax.rsqrt(jnp.mean(gated * gated, axis=-1, keepdims=True) + norm_eps)
        * gate_gain[None, :]
    )


def layer_forward(layer_in, weights, small_params, seq_starts):
    gate_full, conv_full, out_full = weights
    count, span, width = layer_in.shape
    stream = layer_in.reshape(count * span, width).astype(jnp.float32)
    normed = norm_map(stream, small_params[0]).astype(jnp.bfloat16)
    conv_part = jnp.dot(normed, conv_full, preferred_element_type=jnp.float32)
    gate_part = jnp.dot(normed, gate_full, preferred_element_type=jnp.float32)
    mixed = [
        ssd_mix(
            gate_part[m * span : (m + 1) * span],
            conv_part[m * span : (m + 1) * span],
            seq_starts[m],
            *small_params[1:],
        ).astype(jnp.bfloat16)
        for m in range(count)
    ]
    mixed = jnp.concatenate(mixed, 0)
    result = (stream + jnp.dot(mixed, out_full, preferred_element_type=jnp.float32)).astype(
        jnp.bfloat16
    )
    return result.reshape(layer_in.shape), (normed, gate_part, conv_part, mixed)


def layer_backward(layer_in, kept, weights, small_params, seq_starts, upstream):
    normed, gate_part, conv_part, mixed = kept
    gate_full, conv_full, out_full = weights
    count, span, width = layer_in.shape
    upstream = upstream.reshape(count * span, width)
    upstream_bf = upstream.astype(jnp.bfloat16)
    grad_mixed = jnp.dot(upstream_bf, out_full.T, preferred_element_type=jnp.float32)
    pulled = []
    for m in range(count):
        rows = slice(m * span, (m + 1) * span)

        def mixer_only(gate, conv, *small):
            return ssd_mix(gate, conv, seq_starts[m], *small)

        _, pull = jax.vjp(mixer_only, gate_part[rows], conv_part[rows], *small_params[1:])
        pulled.append(pull(grad_mixed[rows]))
    grad_gate = jnp.concatenate([p[0].astype(jnp.bfloat16) for p in pulled], 0)
    grad_conv = jnp.concatenate([p[1].astype(jnp.bfloat16) for p in pulled], 0)
    grad_small = tuple(sum(p[2 + i] for p in pulled) for i in range(6))
    dims = (((1,), (1,)), ((), ()))
    grad_normed = lax.dot_general(
        grad_gate, gate_full, dims, preferred_element_type=jnp.float32
    ) + lax.dot_general(grad_conv, conv_full, dims, preferred_element_type=jnp.float32)
    stream = layer_in.reshape(count * span, width).astype(jnp.float32)
    _, norm_pull = jax.vjp(norm_map, stream, small_params[0])
    grad_stream, grad_gain = norm_pull(grad_normed)
    grad_in = (upstream + grad_stream).reshape(layer_in.shape)
    return grad_in, (upstream_bf, grad_gate, grad_conv), (grad_gain,) + grad_small


def body(
    tokens,
    cotangent,
    in_weight,
    out_weight,
    norm_gain,
    conv_weight,
    conv_bias,
    step_bias,
    decay_log,
    skip_gain,
    gate_gain,
    seq_starts,
):
    is_first = lax.axis_index("section") == 0
    grid = Grid(lax.axis_size("fsdp"))
    small_params = tuple(
        p[0]
        for p in (norm_gain, conv_weight, conv_bias, step_bias, decay_log, skip_gain, gate_gain)
    )

    def choose(first_val, second_val):
        return jax.tree.map(lambda a, b: jnp.where(is_first, a, b), first_val, second_val)

    def swap(v):
        return lax.ppermute(v, "section", [(0, 1), (1, 0)])

    conv_full = grid.gather(in_weight[0, :, INNER:])
    gate_full = grid.gather(in_weight[0, :, :INNER], light=True)
    out_full = grid.gather(out_weight[0], light=True)
    weights = (gate_full, conv_full, out_full)

    out_a, kept_a = layer_forward(tokens, weights, small_params, seq_starts)
    in_b = swap(out_a)
    out_b, kept_b = layer_forward(in_b, weights, small_params, seq_starts)
    layer_out = choose(out_a, out_b)

    grad_b, back_b, small_b = layer_backward(
        in_b, kept_b, weights, small_params, seq_starts, cotangent
    )
    upstream_a = swap(grad_b.astype(jnp.bfloat16)).astype(jnp.float32)
    grad_a, back_a, small_a = layer_backward(
        tokens, kept_a, weights, small_params, seq_starts, upstream_a
    )
    in_grad = choose(grad_a, grad_b)

    mixed = choose(kept_a[3], kept_b[3])
    normed = choose(kept_a[0], kept_b[0])
    upstream_bf, grad_gate, grad_conv = choose(back_a, back_b)
    out_shard = grid.scatter(mixed.T, upstream_bf, out_weight.shape[1])
    normed_t = normed.T
    gate_shard = grid.scatter(normed_t, grad_gate, in_weight.shape[1])
    conv_shard = grid.scatter(normed_t, grad_conv, in_weight.shape[1])
    in_shard = jnp.concatenate([gate_shard, conv_shard], axis=1)

    small = choose(small_a, small_b)
    sizes = [p.size for p in small]
    packed = grid.total(jnp.concatenate([p.reshape(-1) for p in small]))
    summed, at = [], 0
    for p, size in zip(small, sizes):
        summed.append(packed[at : at + size].reshape(p.shape)[None])
        at += size
    return (layer_out[None], in_grad[None], in_shard[None], out_shard[None], *summed)


def solution(mesh):
    return jax.shard_map(
        body,
        mesh=mesh,
        in_specs=(
            P(None, "fsdp", None),
            P(None, "fsdp", None),
            P("section", "fsdp", None),
            P("section", "fsdp", None),
            P("section", None),
            P("section", None, None),
            P("section", None),
            P("section", None),
            P("section", None),
            P("section", None),
            P("section", None),
            P(None, "fsdp"),
        ),
        out_specs=(
            P("section", None, "fsdp", None),
            P("section", None, "fsdp", None),
            P("section", "fsdp", None),
            P("section", "fsdp", None),
            P("section", None),
            P("section", None, None),
            P("section", None),
            P("section", None),
            P("section", None),
            P("section", None),
            P("section", None),
        ),
        check_vma=False,
    )
```
